1024 devices in a mesh: exp: 32 (over y, z_hi, core), seq: 8 (over x), dp: 4 (over z_lo).
Axes of the slice: x: 8, y: 8, z: 8 (z_hi: 2, z_lo: 4; z = z_hi * 4 + z_lo), core: 2. Of those that a mesh axis runs over, the one named last changes fastest.
Arguments:
- queries: bfloat16 [32, 1024, 4, 2048], P('exp', None, 'dp', 'seq'), may hold values from -160 to 160
- latent_rows: bfloat16 [32, 1024, 512], P('exp'), may hold values from -8 to 8
- key_weight: bfloat16 [512, 4, 2048], P(None, 'dp', 'seq'), may hold values from -1 to 1
- output_grad: bfloat16 [32, 1024, 4, 2048], P('exp', 'seq', 'dp'), may hold values from -6 to 6
- down_weight: bfloat16 [32, 2048, 7168], P('exp', 'dp', 'seq'), may hold values from -0.125 to 0.125
- hidden_rows: bfloat16 [6144, 2048], P('exp', 'dp'), may hold values from -6 to 6
- upstream_rows: bfloat16 [6144, 7168], P('exp', 'seq'), may hold values from -6 to 6
- row_gates: float32 [6144], P('exp'), may hold values from 0.03 to 0.5
- row_counts: int32 [32, 3], P('exp'), may hold values from 0 to 64, as said below
Outputs:
- value_grad: bfloat16 [32, 1024, 4, 2048], P('exp', None, 'dp', 'seq')
- hidden_grad: float32 [6144, 2048], P(('exp', 'seq'), 'dp')
- weight_grad: bfloat16 [32, 2048, 7168], P('exp', 'dp', 'seq')
The draws below stay inside these ranges and needn't reach their ends.
Inputs may be any that keep to these rules, and one draw needn't show every extreme that they name: `row_counts`: A block with 0 live rows means host j keeps no copy of expert e(j, b); in every draw some block is full with 64 live rows.
All inputs are finite; a program needn't handle non-finite values.
Results may differ from the reference program's by a relative error of at most 0.012.
The reference program's roundings to bfloat16 on the way count: a program that leaves them out, or rounds other values in their place, can miss the bound.
Values may be sent and summed in bfloat16 or wider, within the bound.
No kernel may reach another device: no remote copies, remote signals or barrier semaphores. Data moves between devices by JAX's collectives and lax.ppermute only.
A program may use at most 32 MiB of HBM per device.

```python
import math
import jax
import jax.numpy as jnp
from jax import lax

D = 7168
FF = 2048
HEADS = 64
HEAD_DIM = 128
LATENT = 512
CAP = 64
EXPERTS = 32
SEQS = 32
S_LEN = 1024
STRIDE = 10
ROWS = 6144
N_DP = 4


def attention_draws(key):
    latent_key = jax.random.fold_in(key, 101)
    weight_key = jax.random.fold_in(key, 102)
    query_key = jax.random.fold_in(key, 103)
    group_width = HEADS // N_DP * HEAD_DIM
    latent_draw = jnp.clip(jax.random.normal(latent_key, (SEQS, S_LEN, LATENT), jnp.float32), -6.0, 6.0)
    projection = jnp.clip(jax.random.normal(weight_key, (LATENT, N_DP, group_width), jnp.float32), -6.0, 6.0) / math.sqrt(LATENT)
    query_draw = jnp.clip(jax.random.normal(query_key, (SEQS, S_LEN, N_DP, group_width), jnp.float32), -6.0, 6.0)
    return (latent_draw, projection, query_draw)


def draw_queries(key, part):
    return attention_draws(key)[2].astype(jnp.bfloat16)


def draw_latent_rows(key, part):
    return attention_draws(key)[0].astype(jnp.bfloat16)


def draw_key_weight(key, part):
    return attention_draws(key)[1].astype(jnp.bfloat16)


def draw_row_counts(key, part):
    base_key = jax.random.fold_in(key, 201)
    full_key = jax.random.fold_in(key, 202)
    empty_key = jax.random.fold_in(key, 203)
    host_key = jax.random.fold_in(key, 204)
    base_counts = jax.random.randint(base_key, (EXPERTS, 3), CAP // 4, CAP // 2 + 1)
    full_block = jax.random.randint(full_key, (EXPERTS, 3), 0, 8) == 0
    empty_block = (jax.random.randint(empty_key, (EXPERTS, 3), 0, 4) == 0) & (jnp.arange(3)[None, :] > 0)
    counts_drawn = jnp.where(full_block, CAP, base_counts)
    counts_drawn = jnp.where(empty_block, 0, counts_drawn)
    chosen_host = jax.random.randint(host_key, (), 0, EXPERTS)
    return counts_drawn.at[chosen_host, 0].set(CAP).astype(jnp.int32)


def block_levels(rng, shape, cuts, low, top_value):
    factor_of, own = 1.0, jax.random.fold_in(rng, 6)
    for dim, blocks in cuts:
        draws = jnp.exp(jax.random.uniform(jax.random.fold_in(own, dim), (blocks,), jnp.float32, low / len(cuts), top_value / len(cuts)))
        factor_of = factor_of * jnp.repeat(draws, shape[dim] // blocks).reshape([-1 if axis == dim else 1 for axis in range(len(shape))])
    return factor_of


def centred(rng, dims, spread, limit, cuts=(), kind=jnp.bfloat16):
    drawn = spread * jax.random.normal(rng, dims, jnp.float32)
    if cuts:
        drawn = drawn * block_levels(rng, dims, cuts, -0.22, 0.18)
    return jnp.clip(drawn, -limit, limit).astype(kind)


def setup_inputs(seed: int = 0) -> dict:
    splits = jax.random.split(jax.random.key(seed), 10)
    queries = draw_queries(jax.random.fold_in(splits[9], 71), 0)
    latent_rows = draw_latent_rows(jax.random.fold_in(splits[9], 71), 0)
    key_weight = draw_key_weight(jax.random.fold_in(splits[9], 71), 0)
    output_grad = centred(splits[3], (SEQS, S_LEN, N_DP, HEADS // N_DP * HEAD_DIM), 1.0, 6.0, ((0, 32), (1, 8), (2, 4)))
    down_weight = centred(splits[4], (EXPERTS, FF, D), FF ** -0.5, 0.125, ((0, 32), (1, 4), (2, 8)))
    hidden_rows = centred(splits[5], (ROWS, FF), 1.0, 6.0, ((0, 32), (1, 4)))
    upstream_rows = centred(splits[6], (ROWS, D), 1.0, 6.0, ((0, 32), (1, 8)))
    row_gates = jnp.clip(jnp.exp(math.log(0.5) - 2.8134107 * jax.random.uniform(splits[7], (ROWS,), jnp.float32) ** block_levels(splits[7], (ROWS,), ((0, 32),), -0.2, 0.2)), 0.03, 0.5)
    row_counts = draw_row_counts(jax.random.fold_in(splits[9], 71), 0)
    return dict(queries=queries, latent_rows=latent_rows, key_weight=key_weight, output_grad=output_grad, down_weight=down_weight, hidden_rows=hidden_rows, upstream_rows=upstream_rows, row_gates=row_gates, row_counts=row_counts)


def one_head(inputs):
    query_head, key_head, grad_head = inputs
    score_scale = 1.0 / math.sqrt(HEAD_DIM)
    scores = jnp.dot(query_head, key_head.T, preferred_element_type=jnp.float32) * score_scale
    positions = jnp.arange(S_LEN)
    allowed = positions[None, :] <= positions[:, None]
    scores = jnp.where(allowed, scores, -jnp.inf)
    row_max = lax.optimization_barrier(jnp.max(scores, axis=1, keepdims=True))
    weights = jnp.exp(scores - row_max)
    softmax_rows = (weights / lax.optimization_barrier(jnp.sum(weights, axis=1, keepdims=True))).astype(jnp.bfloat16)
    return jnp.dot(softmax_rows.T, grad_head, preferred_element_type=jnp.float32).astype(jnp.bfloat16)

def attention_reference(queries, latent_rows, key_weight, output_grad):
    key_matrix = key_weight.reshape(LATENT, HEADS * HEAD_DIM)

    def one_sequence(inputs):
        latent_seq, query_seq, grad_seq = inputs
        key_rows = jnp.dot(latent_seq, key_matrix, preferred_element_type=jnp.float32).astype(jnp.bfloat16)
        key_heads = key_rows.reshape(S_LEN, HEADS, HEAD_DIM).transpose(1, 0, 2)
        query_heads = query_seq.reshape(S_LEN, HEADS, HEAD_DIM).transpose(1, 0, 2)
        grad_heads = grad_seq.reshape(S_LEN, HEADS, HEAD_DIM).transpose(1, 0, 2)
        result = lax.map(one_head, (query_heads, key_heads, grad_heads))
        return result.transpose(1, 0, 2).reshape(S_LEN, HEADS * HEAD_DIM)
    value_grad = lax.map(one_sequence, (latent_rows, queries.reshape(SEQS, S_LEN, HEADS * HEAD_DIM), output_grad.reshape(SEQS, S_LEN, HEADS * HEAD_DIM)))
    return value_grad.reshape(SEQS, S_LEN, N_DP, HEADS // N_DP * HEAD_DIM)

def expert_reference(down_weight, hidden_rows, upstream_rows, row_gates, row_counts):
    host_ids = jnp.arange(EXPERTS, dtype=jnp.int32)
    live_rows = jnp.arange(CAP, dtype=jnp.int32)[None, None, :] < row_counts[:, :, None]
    row_scale = jnp.where(live_rows, row_gates.reshape(EXPERTS, 3, CAP), jnp.zeros((), row_gates.dtype))
    hidden_blocks = hidden_rows.reshape(EXPERTS, 3, CAP, FF)
    upstream_blocks = upstream_rows.reshape(EXPERTS, 3, CAP, D)
    scaled_rows = (row_scale[..., None] * hidden_blocks.astype(jnp.float32)).astype(jnp.bfloat16)

    def host_grad(inputs):
        host_index, upstream_host, scale_host = inputs
        pieces = []
        for block_index in range(3):
            expert = (host_index - block_index * STRIDE) % EXPERTS
            matrix = lax.dynamic_index_in_dim(down_weight, expert, 0, keepdims=False)
            product = jnp.dot(upstream_host[block_index], matrix.T, preferred_element_type=jnp.float32)
            pieces.append(product * scale_host[block_index][:, None])
        return jnp.concatenate(pieces, 0)
    hidden_grad = lax.map(host_grad, (host_ids, upstream_blocks, row_scale)).reshape(ROWS, FF)

    def expert_grad(expert):
        summed = jnp.zeros((FF, D), jnp.float32)
        for block_index in range(3):
            host_index = (expert + block_index * STRIDE) % EXPERTS
            chosen_rows = lax.dynamic_index_in_dim(scaled_rows, host_index, 0, keepdims=False)[block_index]
            upstream = lax.dynamic_index_in_dim(upstream_blocks, host_index, 0, keepdims=False)[block_index]
            block_term = jnp.dot(chosen_rows.T, upstream, preferred_element_type=jnp.float32).astype(jnp.bfloat16)
            summed = summed + lax.optimization_barrier(block_term).astype(jnp.float32)
        return summed.astype(jnp.bfloat16)
    weight_grad = lax.map(expert_grad, host_ids)
    return (hidden_grad, weight_grad)

def reference(queries, latent_rows, key_weight, output_grad, down_weight, hidden_rows, upstream_rows, row_gates, row_counts):
    value_grad = attention_reference(queries, latent_rows, key_weight, output_grad)
    hidden_grad, weight_grad = expert_reference(down_weight, hidden_rows, upstream_rows, row_gates, row_counts)
    return (value_grad, hidden_grad, weight_grad)
```

```python
import math

import jax
import jax.numpy as jnp
from jax import lax
from jax.experimental import pallas as pl
from jax.experimental.pallas import tpu as pltpu
from jax.sharding import PartitionSpec as P


HEAD_DIM = 128
TILE = 256
NT = (((1,), (1,)), ((), ()))
TN = (((0,), (0,)), ((), ()))
VMEM = pl.BlockSpec(memory_space=pltpu.VMEM)
SMEM = pl.BlockSpec(memory_space=pltpu.SMEM)


def call(body, shapes, specs, **options):
    single = not isinstance(shapes, (list, tuple))
    return pl.pallas_call(
        body,
        out_shape=shapes,
        in_specs=specs,
        out_specs=VMEM if single else tuple(VMEM for _ in shapes),
        compiler_params=pltpu.CompilerParams(vmem_limit_bytes=48 * 1024 * 1024),
        **options,
    )


def pack_body(counts, gates, hidden, upstream, pack1, pack2, own, scales):
    cap = own.shape[0]
    wide = upstream.shape[1]
    rows = lax.broadcasted_iota(jnp.int32, (cap, cap), 0)
    cols = lax.broadcasted_iota(jnp.int32, (cap, cap), 1)
    outs = (None, pack1, pack2)
    for b in range(3):
        gate = gates[0:1, b * cap : (b + 1) * cap]
        chosen = jnp.where((rows == cols) & (rows < counts[0, b]), gate, 0.0)
        scale = jnp.sum(chosen, axis=1, keepdims=True)
        span = slice(b * cap, (b + 1) * cap)
        scaled = (scale * hidden[span, :].astype(jnp.float32)).astype(jnp.bfloat16)
        scales[span, :] = jnp.broadcast_to(scale, (cap, 128))
        if b == 0:
            own[...] = scaled
        else:
            outs[b][:, :wide] = upstream[span, :]
            outs[b][:, wide:] = scaled


def split_body(grads, pieces):
    count, _, width = pieces.shape
    for s in range(count):
        pieces[s] = grads[:, s * width : (s + 1) * width]


def probs_body(latent, key_weight, queries, probs, keys):
    seq_len = latent.shape[0]
    keys[...] = jnp.dot(
        latent[...], key_weight[...], preferred_element_type=jnp.float32
    ).astype(jnp.bfloat16)
    factor = math.log2(math.e) / math.sqrt(HEAD_DIM)
    later = lax.broadcasted_iota(jnp.int32, (TILE, TILE), 0) > lax.broadcasted_iota(
        jnp.int32, (TILE, TILE), 1
    )
    for head in range(queries.shape[1] // HEAD_DIM):
        feats = slice(head * HEAD_DIM, (head + 1) * HEAD_DIM)
        for tile in range(seq_len // TILE):
            start, stop = tile * TILE, (tile + 1) * TILE
            query = queries[start:stop, feats]
            diagonal = lax.dot_general(
                keys[start:stop, feats], query, NT, preferred_element_type=jnp.float32
            )
            diagonal = jnp.where(later, -jnp.inf, diagonal)
            top = jnp.max(diagonal, axis=0, keepdims=True)
            if tile:
                before = lax.dot_general(
                    keys[:start, feats], query, NT, preferred_element_type=jnp.float32
                )
                top = jnp.maximum(top, jnp.max(before, axis=0, keepdims=True))
                before = jnp.exp2((before - top) * factor)
            diagonal = jnp.exp2((diagonal - top) * factor)
            total = jnp.sum(diagonal, axis=0, keepdims=True)
            if tile:
                total = total + jnp.sum(before, axis=0, keepdims=True)
            inverse = 1.0 / total
            probs[head, start:stop, start:stop] = (diagonal * inverse).astype(jnp.bfloat16)
            if tile:
                probs[head, :start, start:stop] = (before * inverse).astype(jnp.bfloat16)


def value_body(probs, grads, out):
    seq_len = grads.shape[0]
    for head in range(grads.shape[1] // HEAD_DIM):
        feats = slice(head * HEAD_DIM, (head + 1) * HEAD_DIM)
        for tile in range(seq_len // TILE):
            start, stop = tile * TILE, (tile + 1) * TILE
            out[start:stop, feats] = jnp.dot(
                probs[head, start:stop, start:],
                grads[start:, feats],
                preferred_element_type=jnp.float32,
            ).astype(jnp.bfloat16)


def partial_body(weight, upstream, first, second, out):
    cap = first.shape[0]
    wide = weight.shape[1]
    matrix = weight[...]
    for b, rows in enumerate((upstream[:cap, :], first[:, :wide], second[:, :wide])):
        out[b * cap : (b + 1) * cap, :] = lax.dot_general(
            rows, matrix, NT, preferred_element_type=jnp.float32
        ).astype(jnp.bfloat16)


def weight_body(upstream, own, first, second, out):
    cap, hid = own.shape
    wide = upstream.shape[1]
    chunk = 128
    for start in range(0, hid, chunk):
        stop = start + chunk
        total = None
        for left, right in (
            (own[:, start:stop], upstream[:cap, :]),
            (first[:, wide + start : wide + stop], first[:, :wide]),
            (second[:, wide + start : wide + stop], second[:, :wide]),
        ):
            term = lax.dot_general(left, right, TN, preferred_element_type=jnp.float32)
            term = term.astype(jnp.bfloat16).astype(jnp.float32)
            total = term if total is None else total + term
        out[start:stop, :] = total.astype(jnp.bfloat16)


def shifted(block, axis, distance):
    devices = range(lax.axis_size(axis))
    route = [(i, (i + distance) % len(devices)) for i in devices]
    return lax.ppermute(block, axis, route)


def on_device(
    queries,
    latent_rows,
    key_weight,
    output_grad,
    down_weight,
    hidden_rows,
    upstream_rows,
    row_gates,
    row_counts,
):
    n_seq = lax.axis_size("seq")
    n_exp = lax.axis_size("exp")
    step = n_exp // 3
    rows, hid = hidden_rows.shape
    cap = rows // 3
    own_rows = rows // n_seq
    wide = upstream_rows.shape[1]
    seq_len, width = queries.shape[1], queries.shape[3]
    tokens = output_grad.shape[1]
    bf16, f32 = jnp.bfloat16, jnp.float32

    pack1, pack2, own, scales = call(
        pack_body,
        [
            jax.ShapeDtypeStruct((cap, wide + hid), bf16),
            jax.ShapeDtypeStruct((cap, wide + hid), bf16),
            jax.ShapeDtypeStruct((cap, hid), bf16),
            jax.ShapeDtypeStruct((rows, 128), f32),
        ],
        [SMEM, VMEM, VMEM, VMEM],
        name="pack",
    )(row_counts, row_gates.reshape(1, rows), hidden_rows, upstream_rows)
    first = shifted(pack1, "exp", -step)
    second = shifted(pack2, "exp", -2 * step)

    pack1, pack2, output_grad = lax.optimization_barrier((pack1, pack2, output_grad))
    pieces = call(
        split_body, jax.ShapeDtypeStruct((n_seq, tokens, width), bf16), [VMEM], name="split"
    )(output_grad.reshape(tokens, n_seq * width))
    head_grads = lax.all_to_all(pieces, "seq", split_axis=0, concat_axis=0, tiled=True)

    probs = call(
        probs_body,
        jax.ShapeDtypeStruct((width // HEAD_DIM, seq_len, seq_len), bf16),
        [VMEM, VMEM, VMEM],
        scratch_shapes=[pltpu.VMEM((seq_len, width), bf16)],
        name="probs",
    )(
        latent_rows[0],
        key_weight.reshape(key_weight.shape[0], width),
        queries.reshape(seq_len, width),
    )

    first, second, head_grads, probs = lax.optimization_barrier(
        (first, second, head_grads, probs)
    )
    parts = call(
        partial_body, jax.ShapeDtypeStruct((rows, hid), bf16), [VMEM] * 4, name="parts"
    )(down_weight[0], upstream_rows, first, second)
    shares = lax.all_to_all(
        parts.reshape(n_seq, own_rows, hid), "seq", split_axis=0, concat_axis=0, tiled=True
    )

    weight_grad = call(
        weight_body, jax.ShapeDtypeStruct((hid, wide), bf16), [VMEM] * 4, name="weight"
    )(upstream_rows, own, first, second)[None]
    value_grad = call(
        value_body, jax.ShapeDtypeStruct((seq_len, width), bf16), [VMEM] * 2, name="value"
    )(probs, head_grads.reshape(seq_len, width)).reshape(queries.shape)

    shares, weight_grad = lax.optimization_barrier((shares, weight_grad))

    summed = jnp.sum(shares.astype(f32), axis=0)
    needs = [
        [b for b in (1, 2) if s * own_rows < (b + 1) * cap and (s + 1) * own_rows > b * cap]
        for s in range(n_seq)
    ]
    backs = []
    for turn in range(2):
        route = [
            (e * n_seq + s, (e + blocks[turn] * step) % n_exp * n_seq + s)
            for s, blocks in enumerate(needs)
            if turn < len(blocks)
            for e in range(n_exp)
        ]
        backs.append(lax.ppermute(summed, ("exp", "seq"), route))
    row_start = lax.axis_index("seq") * own_rows
    block_ids = ((row_start + jnp.arange(own_rows)) // cap)[:, None]
    second_of_two = (block_ids == 2) & (row_start // cap == 1)
    total = jnp.where(block_ids == 0, summed, jnp.where(second_of_two, backs[1], backs[0]))
    own_scale = lax.dynamic_slice(scales, (row_start, 0), (own_rows, 1))
    hidden_grad = total * own_scale
    return (value_grad, hidden_grad, weight_grad)


def solution(mesh):
    placed = (
        P("exp", None, "dp", "seq"),
        P("exp", None, None),
        P(None, "dp", "seq"),
        P("exp", "seq", "dp", None),
        P("exp", "dp", "seq"),
        P("exp", "dp"),
        P("exp", "seq"),
        P("exp"),
        P("exp", None),
    )
    return jax.shard_map(
        on_device,
        mesh=mesh,
        in_specs=placed,
        out_specs=(P("exp", None, "dp", "seq"), P(("exp", "seq"), "dp"), P("exp", "dp", "seq")),
        check_vma=False,
    )
```

```python
import math

import jax
import jax.numpy as jnp
from jax import lax
from jax.experimental import pallas as pl
from jax.experimental.pallas import tpu as pltpu
from jax.sharding import PartitionSpec as P


HEAD_DIM = 128
TILE = 256
NT = (((1,), (1,)), ((), ()))
TN = (((0,), (0,)), ((), ()))
VMEM = pl.BlockSpec(memory_space=pltpu.VMEM)
HBM = pl.BlockSpec(memory_space=pltpu.HBM)


def call(body, shapes, specs, outs=VMEM, limit=12, **options):
    single = not isinstance(shapes, (list, tuple))
    return pl.pallas_call(
        body,
        out_shape=shapes,
        in_specs=specs,
        out_specs=outs if single else tuple(outs for _ in shapes),
        compiler_params=pltpu.CompilerParams(vmem_limit_bytes=limit * 1024 * 1024),
        **options,
    )


def in_hbm(array):
    return pltpu.with_memory_space_constraint(array, pltpu.HBM)


def cut_body(upstream, grads, near, far, pieces, sems):
    cap = near.shape[0]
    count, _, width = pieces.shape
    copies = [
        pltpu.make_async_copy(upstream.at[pl.ds(cap, cap), :], near, sems.at[0]),
        pltpu.make_async_copy(upstream.at[pl.ds(2 * cap, cap), :], far, sems.at[1]),
    ]
    for s in range(count):
        copies.append(
            pltpu.make_async_copy(
                grads.at[:, pl.ds(s * width, width)], pieces.at[s], sems.at[2 + s]
            )
        )
    for copy in copies:
        copy.start()
    for copy in copies:
        copy.wait()


def scale_body(counts, gates, hidden, own, near, far, scales, counts_s, gates_v, hidden_v, sems):
    cap = own.shape[0]
    loads = [
        pltpu.make_async_copy(source, target, sems.at[index])
        for index, (source, target) in enumerate(
            ((counts, counts_s), (gates, gates_v), (hidden, hidden_v))
        )
    ]
    for load in loads:
        load.start()
    for load in loads:
        load.wait()
    rows = lax.broadcasted_iota(jnp.int32, (cap, cap), 0)
    cols = lax.broadcasted_iota(jnp.int32, (cap, cap), 1)
    for b, out in enumerate((own, near, far)):
        gate = gates_v[0:1, b * cap : (b + 1) * cap]
        chosen = jnp.where((rows == cols) & (rows < counts_s[0, b]), gate, 0.0)
        scale = jnp.sum(chosen, axis=1, keepdims=True)
        span = slice(b * cap, (b + 1) * cap)
        out[...] = (scale * hidden_v[span, :].astype(jnp.float32)).astype(jnp.bfloat16)
        scales[span, :] = jnp.broadcast_to(scale, (cap, 128))


def probs_body(latent, key_weight, queries, probs, latent_v, weight_v, query_v, keys, tiles, sems, out_sems):
    seq_len = latent.shape[0]
    count = seq_len // TILE
    loads = [
        pltpu.make_async_copy(key_weight, weight_v, sems.at[0]),
        pltpu.make_async_copy(queries, query_v, sems.at[1]),
    ]
    for tile in range(count):
        span = pl.ds(tile * TILE, TILE)
        loads.append(
            pltpu.make_async_copy(latent.at[span, :], latent_v.at[span, :], sems.at[2 + tile])
        )
    for index in (0, 2, 1, *range(3, 2 + count)):
        loads[index].start()
    factor = math.log2(math.e) / math.sqrt(HEAD_DIM)
    later = lax.broadcasted_iota(jnp.int32, (TILE, TILE), 0) > lax.broadcasted_iota(
        jnp.int32, (TILE, TILE), 1
    )
    stores = []
    loads[0].wait()
    for tile in range(count):
        start, stop = tile * TILE, (tile + 1) * TILE
        loads[2 + tile].wait()
        keys[start:stop, :] = jnp.dot(
            latent_v[start:stop, :], weight_v[...], preferred_element_type=jnp.float32
        ).astype(jnp.bfloat16)
        if tile == 0:
            loads[1].wait()
        for head in range(queries.shape[1] // HEAD_DIM):
            feats = slice(head * HEAD_DIM, (head + 1) * HEAD_DIM)
            query = query_v[start:stop, feats]
            diagonal = lax.dot_general(
                keys[start:stop, feats], query, NT, preferred_element_type=jnp.float32
            )
            diagonal = jnp.where(later, -jnp.inf, diagonal)
            top = jnp.max(diagonal, axis=0, keepdims=True)
            if tile:
                before = lax.dot_general(
                    keys[:start, feats], query, NT, preferred_element_type=jnp.float32
                )
                top = jnp.maximum(top, jnp.max(before, axis=0, keepdims=True))
                before = jnp.exp2((before - top) * factor)
            diagonal = jnp.exp2((diagonal - top) * factor)
            total = jnp.sum(diagonal, axis=0, keepdims=True)
            if tile:
                total = total + jnp.sum(before, axis=0, keepdims=True)
            inverse = 1.0 / total
            tiles[head, start:stop, start:stop] = (diagonal * inverse).astype(jnp.bfloat16)
            if tile:
                tiles[head, :start, start:stop] = (before * inverse).astype(jnp.bfloat16)
            area = (head, pl.ds(0, stop), pl.ds(start, TILE))
            stores.append(
                pltpu.make_async_copy(
                    tiles.at[area], probs.at[area], out_sems.at[head * count + tile]
                )
            )
            stores[-1].start()
    for store in stores:
        store.wait()


def value_body(probs, grads, out, tiles, sems):
    seq_len = grads.shape[0]
    count = seq_len // TILE
    heads = grads.shape[1] // HEAD_DIM
    loads = []
    for head in range(heads):
        for tile in range(count):
            area = (head, pl.ds(0, (tile + 1) * TILE), pl.ds(tile * TILE, TILE))
            loads.append(
                pltpu.make_async_copy(probs.at[area], tiles.at[area], sems.at[head * count + tile])
            )
    for load in loads:
        load.start()
    for head in range(heads):
        feats = slice(head * HEAD_DIM, (head + 1) * HEAD_DIM)
        for tile in range(count):
            loads[head * count + tile].wait()
        for tile in range(count):
            start, stop = tile * TILE, (tile + 1) * TILE
            out[start:stop, feats] = jnp.dot(
                tiles[head, start:stop, start:],
                grads[start:, feats],
                preferred_element_type=jnp.float32,
            ).astype(jnp.bfloat16)


def partial_body(weight, upstream, near, far, own_out, near_out, far_out):
    cap = near.shape[0]
    matrix = weight[...]
    for rows, out in ((near[...], near_out), (far[...], far_out), (upstream[:cap, :], own_out)):
        out[...] = lax.dot_general(
            rows, matrix, NT, preferred_element_type=jnp.float32
        ).astype(jnp.bfloat16)


def weight_body(upstream, own, near_rows, near, far_rows, far, out):
    cap, hid = own.shape
    chunk = 128
    for start in range(0, hid, chunk):
        feats = slice(start, start + chunk)
        total = None
        for left, right in (
            (own[:, feats], upstream[:cap, :]),
            (near[:, feats], near_rows[...]),
            (far[:, feats], far_rows[...]),
        ):
            term = lax.dot_general(left, right, TN, preferred_element_type=jnp.float32)
            term = term.astype(jnp.bfloat16).astype(jnp.float32)
            total = term if total is None else total + term
        out[feats, :] = total.astype(jnp.bfloat16)


def shifted(block, axis, distance):
    devices = range(lax.axis_size(axis))
    route = [(i, (i + distance) % len(devices)) for i in devices]
    return lax.ppermute(block, axis, route)


def on_device(
    queries,
    latent_rows,
    key_weight,
    output_grad,
    down_weight,
    hidden_rows,
    upstream_rows,
    row_gates,
    row_counts,
):
    n_seq = lax.axis_size("seq")
    n_exp = lax.axis_size("exp")
    step = n_exp // 3
    rows, hid = hidden_rows.shape
    cap = rows // 3
    own_rows = rows // n_seq
    wide = upstream_rows.shape[1]
    seq_len, width = queries.shape[1], queries.shape[3]
    tokens = output_grad.shape[1]
    bf16, f32 = jnp.bfloat16, jnp.float32

    def shape(*dims, kind=bf16):
        return jax.ShapeDtypeStruct(dims, kind)

    up_near, up_far, pieces = call(
        cut_body,
        [shape(cap, wide), shape(cap, wide), shape(n_seq, tokens, width)],
        [HBM, HBM],
        outs=HBM,
        scratch_shapes=[pltpu.SemaphoreType.DMA((2 + n_seq,))],
        name="cut",
    )(in_hbm(upstream_rows), in_hbm(output_grad.reshape(tokens, n_seq * width)))
    up_near = shifted(up_near, "exp", -step)
    up_far = shifted(up_far, "exp", -2 * step)
    head_grads = lax.all_to_all(pieces, "seq", split_axis=0, concat_axis=0, tiled=True)

    own, near, far, scales = call(
        scale_body,
        [shape(cap, hid)] * 3 + [shape(rows, 128, kind=f32)],
        [HBM, HBM, HBM],
        scratch_shapes=[
            pltpu.SMEM((1, 3), jnp.int32),
            pltpu.VMEM((1, rows), f32),
            pltpu.VMEM((rows, hid), bf16),
            pltpu.SemaphoreType.DMA((3,)),
        ],
        name="scale",
    )(in_hbm(row_counts), in_hbm(row_gates.reshape(1, rows)), in_hbm(hidden_rows))
    near = shifted(near, "exp", -step)
    far = shifted(far, "exp", -2 * step)

    heads = width // HEAD_DIM
    count = seq_len // TILE
    probs = call(
        probs_body,
        pltpu.HBM((heads, seq_len, seq_len), bf16),
        [HBM, HBM, HBM],
        outs=HBM,
        scratch_shapes=[
            pltpu.VMEM(latent_rows.shape[1:], bf16),
            pltpu.VMEM((key_weight.shape[0], width), bf16),
            pltpu.VMEM((seq_len, width), bf16),
            pltpu.VMEM((seq_len, width), bf16),
            pltpu.VMEM((heads, seq_len, seq_len), bf16),
            pltpu.SemaphoreType.DMA((2 + count,)),
            pltpu.SemaphoreType.DMA((heads * count,)),
        ],
        limit=20,
        name="probs",
    )(
        in_hbm(latent_rows[0]),
        in_hbm(key_weight.reshape(key_weight.shape[0], width)),
        in_hbm(queries.reshape(seq_len, width)),
    )
    up_near, up_far, probs = lax.optimization_barrier((up_near, up_far, probs))

    part_own, part_near, part_far = call(
        partial_body, [shape(cap, hid)] * 3, [VMEM] * 4, name="parts"
    )(down_weight[0], upstream_rows, up_near, up_far)
    part_near = shifted(part_near, "exp", step)
    part_far = shifted(part_far, "exp", 2 * step)
    parts = jnp.concatenate([part_own, part_near, part_far], axis=0)
    shares = lax.all_to_all(
        parts.reshape(n_seq, own_rows, hid), "seq", split_axis=0, concat_axis=0, tiled=True
    )
    weight_grad = call(weight_body, shape(hid, wide), [VMEM] * 6, name="weight")(
        upstream_rows, own, up_near, near, up_far, far
    )[None]
    value_grad = call(
        value_body,
        shape(seq_len, width),
        [HBM, VMEM],
        scratch_shapes=[
            pltpu.VMEM((heads, seq_len, seq_len), bf16),
            pltpu.SemaphoreType.DMA((heads * count,)),
        ],
        name="value",
    )(in_hbm(probs), head_grads.reshape(seq_len, width)).reshape(queries.shape)

    row_start = lax.axis_index("seq") * own_rows
    own_scale = lax.dynamic_slice(scales, (row_start, 0), (own_rows, 1))
    hidden_grad = jnp.sum(shares.astype(f32), axis=0) * own_scale
    return (value_grad, hidden_grad, weight_grad)


def solution(mesh):
    placed = (
        P("exp", None, "dp", "seq"),
        P("exp", None, None),
        P(None, "dp", "seq"),
        P("exp", "seq", "dp", None),
        P("exp", "dp", "seq"),
        P("exp", "dp"),
        P("exp", "seq"),
        P("exp"),
        P("exp", None),
    )
    return jax.shard_map(
        on_device,
        mesh=mesh,
        in_specs=placed,
        out_specs=(P("exp", None, "dp", "seq"), P(("exp", "seq"), "dp"), P("exp", "dp", "seq")),
        check_vma=False,
    )
```

```python
import math

import jax
import jax.numpy as jnp
from jax import lax
from jax.experimental import pallas as pl
from jax.experimental.pallas import tpu as pltpu
from jax.sharding import PartitionSpec as P


HEAD_DIM = 128
TILE = 256
CUTS = ((0, 96), (96, 32))
NT = (((1,), (1,)), ((), ()))
TN = (((0,), (0,)), ((), ()))
VMEM = pl.BlockSpec(memory_space=pltpu.VMEM)
HBM = pl.BlockSpec(memory_space=pltpu.HBM)


def call(body, shapes, specs, outs=VMEM, limit=12, **options):
    single = not isinstance(shapes, (list, tuple))
    return pl.pallas_call(
        body,
        out_shape=shapes,
        in_specs=specs,
        out_specs=outs if single else tuple(outs for _ in shapes),
        compiler_params=pltpu.CompilerParams(vmem_limit_bytes=limit * 1024 * 1024),
        **options,
    )


def in_hbm(array):
    return pltpu.with_memory_space_constraint(array, pltpu.HBM)


def pack_body(
    counts, gates, hidden, upstream, near, far, own, scales, counts_s, gates_v, hidden_v, sems
):
    cap = own.shape[0]
    wide = upstream.shape[1]
    sources = (
        (counts, counts_s),
        (gates, gates_v),
        (hidden, hidden_v),
        (upstream.at[pl.ds(cap, cap), :], near.at[:, pl.ds(0, wide)]),
        (upstream.at[pl.ds(2 * cap, cap), :], far.at[:, pl.ds(0, wide)]),
    )
    loads = [
        pltpu.make_async_copy(source, target, sems.at[index])
        for index, (source, target) in enumerate(sources)
    ]
    for load in loads:
        load.start()
    for load in loads:
        load.wait()
    rows = lax.broadcasted_iota(jnp.int32, (cap, cap), 0)
    cols = lax.broadcasted_iota(jnp.int32, (cap, cap), 1)
    for b, out in enumerate((own, near, far)):
        gate = gates_v[0:1, b * cap : (b + 1) * cap]
        chosen = jnp.where((rows == cols) & (rows < counts_s[0, b]), gate, 0.0)
        scale = jnp.sum(chosen, axis=1, keepdims=True)
        span = slice(b * cap, (b + 1) * cap)
        scaled = (scale * hidden_v[span, :].astype(jnp.float32)).astype(jnp.bfloat16)
        if b:
            out[:, wide:] = scaled
        else:
            out[...] = scaled
        scales[span, :] = jnp.broadcast_to(scale, (cap, 128))


def split_body(grads, *refs):
    pieces, (pieces_v, load_sems, store_sems) = refs[: len(CUTS)], refs[len(CUTS) :]
    count, _, width = pieces_v.shape
    loads = [
        pltpu.make_async_copy(
            grads.at[:, pl.ds(s * width, width)], pieces_v.at[s], load_sems.at[s]
        )
        for s in range(count)
    ]
    stores = [
        pltpu.make_async_copy(
            pieces_v.at[s, pl.ds(first, size), :],
            pieces[index].at[s],
            store_sems.at[s * len(CUTS) + index],
        )
        for s in range(count)
        for index, (first, size) in enumerate(CUTS)
    ]
    for load in loads:
        load.start()
    for s, load in enumerate(loads):
        load.wait()
        for store in stores[s * len(CUTS) : (s + 1) * len(CUTS)]:
            store.start()
    for store in stores:
        store.wait()


def probs_body(latent, key_weight, queries, probs, latent_v, weight_v, query_v, keys, tiles, sems, out_sems):
    seq_len = latent.shape[0]
    count = seq_len // TILE
    loads = [
        pltpu.make_async_copy(key_weight, weight_v, sems.at[0]),
        pltpu.make_async_copy(queries, query_v, sems.at[1]),
    ]
    for tile in range(count):
        span = pl.ds(tile * TILE, TILE)
        loads.append(
            pltpu.make_async_copy(latent.at[span, :], latent_v.at[span, :], sems.at[2 + tile])
        )
    for index in (0, 2, 1, *range(3, 2 + count)):
        loads[index].start()
    factor = math.log2(math.e) / math.sqrt(HEAD_DIM)
    later = lax.broadcasted_iota(jnp.int32, (TILE, TILE), 0) > lax.broadcasted_iota(
        jnp.int32, (TILE, TILE), 1
    )
    stores = []
    loads[0].wait()
    for tile in range(count):
        start, stop = tile * TILE, (tile + 1) * TILE
        loads[2 + tile].wait()
        keys[start:stop, :] = jnp.dot(
            latent_v[start:stop, :], weight_v[...], preferred_element_type=jnp.float32
        ).astype(jnp.bfloat16)
        if tile == 0:
            loads[1].wait()
        for head in range(queries.shape[1] // HEAD_DIM):
            feats = slice(head * HEAD_DIM, (head + 1) * HEAD_DIM)
            query = query_v[start:stop, feats]
            diagonal = lax.dot_general(
                keys[start:stop, feats], query, NT, preferred_element_type=jnp.float32
            )
            diagonal = jnp.where(later, -jnp.inf, diagonal)
            top = jnp.max(diagonal, axis=0, keepdims=True)
            if tile:
                before = lax.dot_general(
                    keys[:start, feats], query, NT, preferred_element_type=jnp.float32
                )
                top = jnp.maximum(top, jnp.max(before, axis=0, keepdims=True))
                before = jnp.exp2((before - top) * factor)
            diagonal = jnp.exp2((diagonal - top) * factor)
            total = jnp.sum(diagonal, axis=0, keepdims=True)
            if tile:
                total = total + jnp.sum(before, axis=0, keepdims=True)
            inverse = 1.0 / total
            tiles[head, start:stop, start:stop] = (diagonal * inverse).astype(jnp.bfloat16)
            if tile:
                tiles[head, :start, start:stop] = (before * inverse).astype(jnp.bfloat16)
            area = (head, pl.ds(0, stop), pl.ds(start, TILE))
            stores.append(
                pltpu.make_async_copy(
                    tiles.at[area], probs.at[area], out_sems.at[head * count + tile]
                )
            )
            stores[-1].start()
    for store in stores:
        store.wait()


def value_body(probs, *refs):
    n_cuts = len(CUTS)
    shares, (out, tiles, grads, sems) = refs[:n_cuts], refs[n_cuts:]
    seq_len = grads.shape[0]
    count = seq_len // TILE
    heads = grads.shape[1] // HEAD_DIM
    loads = []
    for head in range(heads):
        for tile in range(count):
            area = (head, pl.ds(0, (tile + 1) * TILE), pl.ds(tile * TILE, TILE))
            loads.append(
                pltpu.make_async_copy(probs.at[area], tiles.at[area], sems.at[head * count + tile])
            )
    for load in loads:
        load.start()
    tokens = sum(size for _, size in CUTS)
    for (first, size), share in zip(CUTS, shares):
        for s in range(share.shape[0]):
            grads[s * tokens + first : s * tokens + first + size, :] = share[s]
    for head in range(heads):
        feats = slice(head * HEAD_DIM, (head + 1) * HEAD_DIM)
        for tile in range(count):
            loads[head * count + tile].wait()
        for tile in range(count):
            start, stop = tile * TILE, (tile + 1) * TILE
            out[start:stop, feats] = jnp.dot(
                tiles[head, start:stop, start:],
                grads[start:, feats],
                preferred_element_type=jnp.float32,
            ).astype(jnp.bfloat16)


def partial_body(weight, upstream, near, far, out):
    cap = near.shape[0]
    wide = weight.shape[1]
    matrix = weight[...]
    for b, rows in enumerate((upstream[:cap, :], near[:, :wide], far[:, :wide])):
        out[b * cap : (b + 1) * cap, :] = lax.dot_general(
            rows, matrix, NT, preferred_element_type=jnp.float32
        ).astype(jnp.bfloat16)


def weight_body(upstream, own, near, far, out):
    cap, hid = own.shape
    wide = upstream.shape[1]
    chunk = 128
    for start in range(0, hid, chunk):
        feats = slice(start, start + chunk)
        packed = slice(wide + start, wide + start + chunk)
        total = None
        for left, right in (
            (own[:, feats], upstream[:cap, :]),
            (near[:, packed], near[:, :wide]),
            (far[:, packed], far[:, :wide]),
        ):
            term = lax.dot_general(left, right, TN, preferred_element_type=jnp.float32)
            term = term.astype(jnp.bfloat16).astype(jnp.float32)
            total = term if total is None else total + term
        out[feats, :] = total.astype(jnp.bfloat16)


def shifted(block, axis, distance):
    devices = range(lax.axis_size(axis))
    route = [(i, (i + distance) % len(devices)) for i in devices]
    return lax.ppermute(block, axis, route)


def on_device(
    queries,
    latent_rows,
    key_weight,
    output_grad,
    down_weight,
    hidden_rows,
    upstream_rows,
    row_gates,
    row_counts,
):
    n_seq = lax.axis_size("seq")
    n_exp = lax.axis_size("exp")
    step = n_exp // 3
    rows, hid = hidden_rows.shape
    cap = rows // 3
    own_rows = rows // n_seq
    wide = upstream_rows.shape[1]
    seq_len, width = queries.shape[1], queries.shape[3]
    tokens = output_grad.shape[1]
    bf16, f32 = jnp.bfloat16, jnp.float32

    def shape(*dims, kind=bf16):
        return jax.ShapeDtypeStruct(dims, kind)

    near, far, own, scales = call(
        pack_body,
        [shape(cap, wide + hid)] * 2 + [shape(cap, hid), shape(rows, 128, kind=f32)],
        [HBM] * 4,
        scratch_shapes=[
            pltpu.SMEM((1, 3), jnp.int32),
            pltpu.VMEM((1, rows), f32),
            pltpu.VMEM((rows, hid), bf16),
            pltpu.SemaphoreType.DMA((5,)),
        ],
        name="pack",
    )(
        in_hbm(row_counts),
        in_hbm(row_gates.reshape(1, rows)),
        in_hbm(hidden_rows),
        in_hbm(upstream_rows),
    )
    near = shifted(near, "exp", -step)
    far = shifted(far, "exp", -2 * step)
    pieces = call(
        split_body,
        [pltpu.HBM((n_seq, size, width), bf16) for _, size in CUTS],
        [HBM],
        outs=HBM,
        scratch_shapes=[
            pltpu.VMEM((n_seq, tokens, width), bf16),
            pltpu.SemaphoreType.DMA((n_seq,)),
            pltpu.SemaphoreType.DMA((n_seq * len(CUTS),)),
        ],
        name="split",
    )(in_hbm(output_grad.reshape(tokens, n_seq * width)))
    head_grads = []
    for piece in pieces:
        head_grads.append(
            lax.all_to_all(piece, "seq", split_axis=0, concat_axis=0, tiled=True)
        )

    heads = width // HEAD_DIM
    count = seq_len // TILE
    probs = call(
        probs_body,
        pltpu.HBM((heads, seq_len, seq_len), bf16),
        [HBM, HBM, HBM],
        outs=HBM,
        scratch_shapes=[
            pltpu.VMEM(latent_rows.shape[1:], bf16),
            pltpu.VMEM((key_weight.shape[0], width), bf16),
            pltpu.VMEM((seq_len, width), bf16),
            pltpu.VMEM((seq_len, width), bf16),
            pltpu.VMEM((heads, seq_len, seq_len), bf16),
            pltpu.SemaphoreType.DMA((2 + count,)),
            pltpu.SemaphoreType.DMA((heads * count,)),
        ],
        limit=20,
        name="probs",
    )(
        in_hbm(latent_rows[0]),
        in_hbm(key_weight.reshape(key_weight.shape[0], width)),
        in_hbm(queries.reshape(seq_len, width)),
    )
    near, far, probs = lax.optimization_barrier((near, far, probs))

    parts = call(partial_body, shape(rows, hid), [VMEM] * 4, name="parts")(
        down_weight[0], upstream_rows, near, far
    )
    shares = lax.all_to_all(
        parts.reshape(n_seq, own_rows, hid), "seq", split_axis=0, concat_axis=0, tiled=True
    )
    weight_grad = call(weight_body, shape(hid, wide), [VMEM] * 4, name="weight")(
        upstream_rows, own, near, far
    )[None]
    value_grad = call(
        value_body,
        shape(seq_len, width),
        [HBM] + [VMEM] * len(CUTS),
        scratch_shapes=[
            pltpu.VMEM((heads, seq_len, seq_len), bf16),
            pltpu.VMEM((seq_len, width), bf16),
            pltpu.SemaphoreType.DMA((heads * count,)),
        ],
        name="value",
    )(in_hbm(probs), *head_grads).reshape(queries.shape)

    summed = jnp.sum(shares.astype(f32), axis=0)
    needs = [
        [b for b in (1, 2) if s * own_rows < (b + 1) * cap and (s + 1) * own_rows > b * cap]
        for s in range(n_seq)
    ]
    backs = []
    for turn in range(2):
        route = [
            (e * n_seq + s, (e + blocks[turn] * step) % n_exp * n_seq + s)
            for s, blocks in enumerate(needs)
            if turn < len(blocks)
            for e in range(n_exp)
        ]
        backs.append(lax.ppermute(summed.astype(bf16), ("exp", "seq"), route).astype(f32))
    row_start = lax.axis_index("seq") * own_rows
    block_ids = ((row_start + jnp.arange(own_rows)) // cap)[:, None]
    second_of_two = (block_ids == 2) & (row_start // cap == 1)
    total = jnp.where(block_ids == 0, summed, jnp.where(second_of_two, backs[1], backs[0]))
    own_scale = lax.dynamic_slice(scales, (row_start, 0), (own_rows, 1))
    hidden_grad = total * own_scale
    return (value_grad, hidden_grad, weight_grad)


def solution(mesh):
    placed = (
        P("exp", None, "dp", "seq"),
        P("exp", None, None),
        P(None, "dp", "seq"),
        P("exp", "seq", "dp", None),
        P("exp", "dp", "seq"),
        P("exp", "dp"),
        P("exp", "seq"),
        P("exp"),
        P("exp", None),
    )
    return jax.shard_map(
        on_device,
        mesh=mesh,
        in_specs=placed,
        out_specs=(P("exp", None, "dp", "seq"), P(("exp", "seq"), "dp"), P("exp", "dp", "seq")),
        check_vma=False,
    )
```

```python
import math

import jax
import jax.numpy as jnp
from jax import lax
from jax.experimental import pallas as pl
from jax.experimental.pallas import tpu as pltpu
from jax.sharding import PartitionSpec as P


HEAD_DIM = 128
TILE = 256
CUTS = ((0, 128),)
NT = (((1,), (1,)), ((), ()))
TN = (((0,), (0,)), ((), ()))
VMEM = pl.BlockSpec(memory_space=pltpu.VMEM)
HBM = pl.BlockSpec(memory_space=pltpu.HBM)


def call(body, shapes, specs, outs=VMEM, limit=12, **options):
    single = not isinstance(shapes, (list, tuple))
    return pl.pallas_call(
        body,
        out_shape=shapes,
        in_specs=specs,
        out_specs=outs if single else tuple(outs for _ in shapes),
        compiler_params=pltpu.CompilerParams(vmem_limit_bytes=limit * 1024 * 1024),
        **options,
    )


def in_hbm(array):
    return pltpu.with_memory_space_constraint(array, pltpu.HBM)


def pack_body(counts, gates, hidden, upstream, grads, *refs):
    n_cuts = len(CUTS)
    near, far, own, scales, *pieces = refs[: 4 + n_cuts]
    counts_s, gates_v, hidden_v, pieces_v, sems, piece_sems, out_sems = refs[4 + n_cuts :]
    cap = own.shape[0]
    wide = upstream.shape[1]
    count, _, width = pieces_v.shape
    sources = (
        (counts, counts_s),
        (gates, gates_v),
        (hidden, hidden_v),
        (upstream.at[pl.ds(cap, cap), :], near.at[:, pl.ds(0, wide)]),
        (upstream.at[pl.ds(2 * cap, cap), :], far.at[:, pl.ds(0, wide)]),
    )
    loads = [
        pltpu.make_async_copy(source, target, sems.at[index])
        for index, (source, target) in enumerate(sources)
    ]
    piece_loads = [
        pltpu.make_async_copy(
            grads.at[:, pl.ds(s * width, width)], pieces_v.at[s], piece_sems.at[s]
        )
        for s in range(count)
    ]
    for load in loads + piece_loads:
        load.start()
    for load in loads:
        load.wait()
    rows = lax.broadcasted_iota(jnp.int32, (cap, cap), 0)
    cols = lax.broadcasted_iota(jnp.int32, (cap, cap), 1)
    for b, out in enumerate((own, near, far)):
        gate = gates_v[0:1, b * cap : (b + 1) * cap]
        chosen = jnp.where((rows == cols) & (rows < counts_s[0, b]), gate, 0.0)
        scale = jnp.sum(chosen, axis=1, keepdims=True)
        span = slice(b * cap, (b + 1) * cap)
        scaled = (scale * hidden_v[span, :].astype(jnp.float32)).astype(jnp.bfloat16)
        if b:
            out[:, wide:] = scaled
        else:
            out[...] = scaled
        scales[span, :] = jnp.broadcast_to(scale, (cap, 128))
    for load in piece_loads:
        load.wait()
    stores = [
        pltpu.make_async_copy(
            pieces_v.at[:, pl.ds(first, size), :], pieces[index], out_sems.at[index]
        )
        for index, (first, size) in enumerate(CUTS)
    ]
    for store in stores:
        store.start()
    for store in stores:
        store.wait()


def probs_body(latent, key_weight, queries, probs, latent_v, weight_v, query_v, keys, tiles, sems, out_sems):
    seq_len = latent.shape[0]
    count = seq_len // TILE
    loads = [
        pltpu.make_async_copy(key_weight, weight_v, sems.at[0]),
        pltpu.make_async_copy(queries, query_v, sems.at[1]),
    ]
    for tile in range(count):
        span = pl.ds(tile * TILE, TILE)
        loads.append(
            pltpu.make_async_copy(latent.at[span, :], latent_v.at[span, :], sems.at[2 + tile])
        )
    for index in (0, 2, 1, *range(3, 2 + count)):
        loads[index].start()
    factor = math.log2(math.e) / math.sqrt(HEAD_DIM)
    later = lax.broadcasted_iota(jnp.int32, (TILE, TILE), 0) > lax.broadcasted_iota(
        jnp.int32, (TILE, TILE), 1
    )
    stores = []
    loads[0].wait()
    for tile in range(count):
        start, stop = tile * TILE, (tile + 1) * TILE
        loads[2 + tile].wait()
        keys[start:stop, :] = jnp.dot(
            latent_v[start:stop, :], weight_v[...], preferred_element_type=jnp.float32
        ).astype(jnp.bfloat16)
        if tile == 0:
            loads[1].wait()
        for head in range(queries.shape[1] // HEAD_DIM):
            feats = slice(head * HEAD_DIM, (head + 1) * HEAD_DIM)
            query = query_v[start:stop, feats]
            diagonal = lax.dot_general(
                keys[start:stop, feats], query, NT, preferred_element_type=jnp.float32
            )
            diagonal = jnp.where(later, -jnp.inf, diagonal)
            top = jnp.max(diagonal, axis=0, keepdims=True)
            if tile:
                before = lax.dot_general(
                    keys[:start, feats], query, NT, preferred_element_type=jnp.float32
                )
                top = jnp.maximum(top, jnp.max(before, axis=0, keepdims=True))
                before = jnp.exp2((before - top) * factor)
            diagonal = jnp.exp2((diagonal - top) * factor)
            total = jnp.sum(diagonal, axis=0, keepdims=True)
            if tile:
                total = total + jnp.sum(before, axis=0, keepdims=True)
            inverse = 1.0 / total
            tiles[head, start:stop, start:stop] = (diagonal * inverse).astype(jnp.bfloat16)
            if tile:
                tiles[head, :start, start:stop] = (before * inverse).astype(jnp.bfloat16)
            area = (head, pl.ds(0, stop), pl.ds(start, TILE))
            stores.append(
                pltpu.make_async_copy(
                    tiles.at[area], probs.at[area], out_sems.at[head * count + tile]
                )
            )
            stores[-1].start()
    for store in stores:
        store.wait()


def value_body(probs, *refs):
    n_cuts = len(CUTS)
    shares, (out, tiles, grads, sems) = refs[:n_cuts], refs[n_cuts:]
    seq_len = grads.shape[0]
    count = seq_len // TILE
    heads = grads.shape[1] // HEAD_DIM
    loads = []
    for head in range(heads):
        for tile in range(count):
            area = (head, pl.ds(0, (tile + 1) * TILE), pl.ds(tile * TILE, TILE))
            loads.append(
                pltpu.make_async_copy(probs.at[area], tiles.at[area], sems.at[head * count + tile])
            )
    for load in loads:
        load.start()
    tokens = sum(size for _, size in CUTS)
    for (first, size), share in zip(CUTS, shares):
        for s in range(share.shape[0]):
            grads[s * tokens + first : s * tokens + first + size, :] = share[s]
    for head in range(heads):
        feats = slice(head * HEAD_DIM, (head + 1) * HEAD_DIM)
        for tile in range(count):
            loads[head * count + tile].wait()
        for tile in range(count):
            start, stop = tile * TILE, (tile + 1) * TILE
            out[start:stop, feats] = jnp.dot(
                tiles[head, start:stop, start:],
                grads[start:, feats],
                preferred_element_type=jnp.float32,
            ).astype(jnp.bfloat16)


def partial_body(weight, upstream, near, far, out):
    cap = near.shape[0]
    wide = weight.shape[1]
    matrix = weight[...]
    for b, rows in enumerate((upstream[:cap, :], near[:, :wide], far[:, :wide])):
        out[b * cap : (b + 1) * cap, :] = lax.dot_general(
            rows, matrix, NT, preferred_element_type=jnp.float32
        ).astype(jnp.bfloat16)


def weight_body(upstream, own, near, far, out):
    cap, hid = own.shape
    wide = upstream.shape[1]
    chunk = 128
    for start in range(0, hid, chunk):
        feats = slice(start, start + chunk)
        packed = slice(wide + start, wide + start + chunk)
        total = None
        for left, right in (
            (own[:, feats], upstream[:cap, :]),
            (near[:, packed], near[:, :wide]),
            (far[:, packed], far[:, :wide]),
        ):
            term = lax.dot_general(left, right, TN, preferred_element_type=jnp.float32)
            term = term.astype(jnp.bfloat16).astype(jnp.float32)
            total = term if total is None else total + term
        out[feats, :] = total.astype(jnp.bfloat16)


def shifted(block, axis, distance):
    devices = range(lax.axis_size(axis))
    route = [(i, (i + distance) % len(devices)) for i in devices]
    return lax.ppermute(block, axis, route)


def on_device(
    queries,
    latent_rows,
    key_weight,
    output_grad,
    down_weight,
    hidden_rows,
    upstream_rows,
    row_gates,
    row_counts,
):
    n_seq = lax.axis_size("seq")
    n_exp = lax.axis_size("exp")
    step = n_exp // 3
    rows, hid = hidden_rows.shape
    cap = rows // 3
    own_rows = rows // n_seq
    wide = upstream_rows.shape[1]
    seq_len, width = queries.shape[1], queries.shape[3]
    tokens = output_grad.shape[1]
    bf16, f32 = jnp.bfloat16, jnp.float32

    def shape(*dims, kind=bf16):
        return jax.ShapeDtypeStruct(dims, kind)

    near, far, own, scales, *pieces = pl.pallas_call(
        pack_body,
        out_shape=[shape(cap, wide + hid)] * 2
        + [shape(cap, hid), shape(rows, 128, kind=f32)]
        + [pltpu.HBM((n_seq, size, width), bf16) for _, size in CUTS],
        in_specs=[HBM] * 5,
        out_specs=[VMEM] * 4 + [HBM] * len(CUTS),
        scratch_shapes=[
            pltpu.SMEM((1, 3), jnp.int32),
            pltpu.VMEM((1, rows), f32),
            pltpu.VMEM((rows, hid), bf16),
            pltpu.VMEM((n_seq, tokens, width), bf16),
            pltpu.SemaphoreType.DMA((5,)),
            pltpu.SemaphoreType.DMA((n_seq,)),
            pltpu.SemaphoreType.DMA((len(CUTS),)),
        ],
        compiler_params=pltpu.CompilerParams(vmem_limit_bytes=12 * 1024 * 1024),
        name="pack",
    )(
        in_hbm(row_counts),
        in_hbm(row_gates.reshape(1, rows)),
        in_hbm(hidden_rows),
        in_hbm(upstream_rows),
        in_hbm(output_grad.reshape(tokens, n_seq * width)),
    )
    near = shifted(near, "exp", -step)
    far = shifted(far, "exp", -2 * step)
    head_grads = []
    for piece in pieces:
        head_grads.append(
            lax.all_to_all(piece, "seq", split_axis=0, concat_axis=0, tiled=True)
        )

    heads = width // HEAD_DIM
    count = seq_len // TILE
    probs = call(
        probs_body,
        pltpu.HBM((heads, seq_len, seq_len), bf16),
        [HBM, HBM, HBM],
        outs=HBM,
        scratch_shapes=[
            pltpu.VMEM(latent_rows.shape[1:], bf16),
            pltpu.VMEM((key_weight.shape[0], width), bf16),
            pltpu.VMEM((seq_len, width), bf16),
            pltpu.VMEM((seq_len, width), bf16),
            pltpu.VMEM((heads, seq_len, seq_len), bf16),
            pltpu.SemaphoreType.DMA((2 + count,)),
            pltpu.SemaphoreType.DMA((heads * count,)),
        ],
        limit=20,
        name="probs",
    )(
        in_hbm(latent_rows[0]),
        in_hbm(key_weight.reshape(key_weight.shape[0], width)),
        in_hbm(queries.reshape(seq_len, width)),
    )
    near, far, probs = lax.optimization_barrier((near, far, probs))

    parts = call(partial_body, shape(rows, hid), [VMEM] * 4, name="parts")(
        down_weight[0], upstream_rows, near, far
    )
    shares = lax.all_to_all(
        parts.reshape(n_seq, own_rows, hid), "seq", split_axis=0, concat_axis=0, tiled=True
    )
    weight_grad = call(weight_body, shape(hid, wide), [VMEM] * 4, name="weight")(
        upstream_rows, own, near, far
    )[None]
    value_grad = call(
        value_body,
        shape(seq_len, width),
        [HBM] + [VMEM] * len(CUTS),
        scratch_shapes=[
            pltpu.VMEM((heads, seq_len, seq_len), bf16),
            pltpu.VMEM((seq_len, width), bf16),
            pltpu.SemaphoreType.DMA((heads * count,)),
        ],
        name="value",
    )(in_hbm(probs), *head_grads).reshape(queries.shape)

    summed = jnp.sum(shares.astype(f32), axis=0)
    needs = [
        [b for b in (1, 2) if s * own_rows < (b + 1) * cap and (s + 1) * own_rows > b * cap]
        for s in range(n_seq)
    ]
    backs = []
    for turn in range(2):
        route = [
            (e * n_seq + s, (e + blocks[turn] * step) % n_exp * n_seq + s)
            for s, blocks in enumerate(needs)
            if turn < len(blocks)
            for e in range(n_exp)
        ]
        backs.append(lax.ppermute(summed.astype(bf16), ("exp", "seq"), route).astype(f32))
    row_start = lax.axis_index("seq") * own_rows
    block_ids = ((row_start + jnp.arange(own_rows)) // cap)[:, None]
    second_of_two = (block_ids == 2) & (row_start // cap == 1)
    total = jnp.where(block_ids == 0, summed, jnp.where(second_of_two, backs[1], backs[0]))
    own_scale = lax.dynamic_slice(scales, (row_start, 0), (own_rows, 1))
    hidden_grad = total * own_scale
    return (value_grad, hidden_grad, weight_grad)


def solution(mesh):
    placed = (
        P("exp", None, "dp", "seq"),
        P("exp", None, None),
        P(None, "dp", "seq"),
        P("exp", "seq", "dp", None),
        P("exp", "dp", "seq"),
        P("exp", "dp"),
        P("exp", "seq"),
        P("exp"),
        P("exp", None),
    )
    return jax.shard_map(
        on_device,
        mesh=mesh,
        in_specs=placed,
        out_specs=(P("exp", None, "dp", "seq"), P(("exp", "seq"), "dp"), P("exp", "dp", "seq")),
        check_vma=False,
    )
```
